512 devices in a mesh: section: 8 (over z_lo, core), tensor: 8 (over y), copy: 8 (over x, z_hi).
Axes of the slice: x: 4, y: 8, z: 8 (z_hi: 2, z_lo: 4; z = z_hi * 4 + z_lo), core: 2. Of those that a mesh axis runs over, the one named last changes fastest.
Arguments:
- visual: bfloat16 [8, 192, 8192], P('copy', ('section', 'tensor')), may hold values from -6 to 6
- w_key: bfloat16 [8, 8192, 1024], P('section', None, 'tensor'), may hold values from -0.0625 to 0.0625
- w_value: bfloat16 [8, 8192, 1024], P('section', None, 'tensor'), may hold values from -0.0625 to 0.0625
- key_gain: bfloat16 [8, 1024], P('section', 'tensor'), may hold values from 0.25 to 1.75
- queries: bfloat16 [8, 8, 128, 8192], P('section', 'copy', None, 'tensor')
- grad_out: bfloat16 [8, 8, 128, 8192], P('section', 'copy', None, 'tensor'), may hold values from -6 to 6
- offsets: int32 [8], P('copy'), may hold values from 0 to 8
- flips: int32 [8], P('copy'), may hold values from 0 to 1
- lengths: int32 [8], P('copy'), may hold values from 32 to 128, as said below
Outputs:
- patch_grad: float32 [256, 8192], P('section', 'tensor')
The draws below stay inside these ranges and needn't reach their ends.
Inputs may be any that keep to these rules, and one draw needn't show every extreme that they name: `lengths`: every length is at least a quarter of 128, and some copy has all 128 tokens live.
All inputs are finite; a program needn't handle non-finite values.
Results may differ from the reference program's by a relative error of at most 0.014.
The reference program's roundings to bfloat16 on the way (of `term`) count: a program that leaves them out, or rounds other values in their place, can miss the bound.
Values may be sent and summed in bfloat16 or wider, within the bound.
No kernel may reach another device: no remote copies, remote signals or barrier semaphores. Data moves between devices by JAX's collectives and lax.ppermute only.
A program may use at most 64 MiB of HBM per device.

```python
import jax
import jax.numpy as jnp
from jax import lax

D = 8192
HD = 128
GROUP = 8
TXT = 128
GW = 24
BW = 32
KV_HEADS = 8
HEADS = 64
LAYERS = 8
COPIES = 8
GH = 8
VIS = 192


def draw_queries(key, part):
    values = jax.random.normal(key, (LAYERS, COPIES, TXT, HEADS * HD), jnp.float32)
    return values.astype(jnp.bfloat16)


def draw_lengths(key, part):
    drawn = jax.random.randint(key, (COPIES,), TXT // 4, TXT + 1, dtype=jnp.int32)
    chosen = jax.random.randint(jax.random.fold_in(key, 7), (), 0, COPIES, dtype=jnp.int32)
    return jnp.where(jnp.arange(COPIES, dtype=jnp.int32) == chosen, TXT, drawn).astype(jnp.int32)


def touch_ends(values, key, low, largest):
    spot = [jax.random.randint(jax.random.fold_in(key, axis), (), 0, length) for axis, length in enumerate(values.shape)]
    longest = values.shape.index(max(values.shape))
    next_to = spot[:longest] + [(spot[longest] + 1) % values.shape[longest]] + spot[longest + 1:]
    return values.at[tuple(spot)].set(low).at[tuple(next_to)].set(largest)


def steps_of(rng, extent, shards, low, top_value):
    loudness = 1.0
    for dim, blocks in shards:
        steps = jax.random.uniform(jax.random.fold_in(jax.random.fold_in(rng, 6), dim), (blocks,), jnp.float32, low / len(shards), top_value / len(shards))
        loudness = loudness * jnp.repeat(jnp.exp(steps), extent[dim] // blocks).reshape((-1,) + (1,) * (len(extent) - 1 - dim))
    return loudness


def normal_values(stream_key, dims, spread, limit, shards=(), kind=jnp.bfloat16):
    result = jax.random.normal(stream_key, dims, jnp.float32) * spread
    if len(shards) > 0:
        result = steps_of(stream_key, dims, shards, -0.22, 0.18) * result
    return jnp.clip(result, min=-limit, max=limit).astype(kind)


def setup_inputs(seed: int = 0) -> dict:
    arg_keys = jax.random.split(jax.random.key(seed), 10)
    return {
        "visual": normal_values(arg_keys[0], (COPIES, VIS, D), 1.0, 6.0, ((0, 8), (1, 64))),
        "w_key": normal_values(arg_keys[1], (LAYERS, D, KV_HEADS * HD), D ** -0.5, 0.0625, ((0, 8), (2, 8))),
        "w_value": normal_values(arg_keys[2], (LAYERS, D, KV_HEADS * HD), D ** -0.5, 0.0625, ((0, 8), (2, 8))),
        "key_gain": jnp.clip(1.0 + 0.15 * jax.random.normal(arg_keys[3], (LAYERS, KV_HEADS * HD), jnp.float32), 0.25, 1.75).astype(jnp.bfloat16),
        "queries": draw_queries(jax.random.fold_in(arg_keys[9], 71), 0),
        "grad_out": normal_values(arg_keys[5], (LAYERS, COPIES, TXT, HEADS * HD), 1.0, 6.0, ((0, 8), (1, 8), (3, 8))),
        "offsets": touch_ends(jax.random.randint(arg_keys[6], (COPIES,), 0, BW - GW + 1), jax.random.fold_in(arg_keys[6], 1), 0, BW - GW).astype(jnp.int32),
        "flips": touch_ends(jax.random.randint(arg_keys[7], (COPIES,), 0, 2), jax.random.fold_in(arg_keys[7], 1), 0, 1).astype(jnp.int32),
        "lengths": draw_lengths(jax.random.fold_in(arg_keys[9], 71), 0),
    }


EPS = 1e-05

def key_norm(raw, gain):
    scale_row = lax.rsqrt(lax.optimization_barrier(jnp.mean(raw * raw, axis=-1, keepdims=True)) + EPS)
    return raw * scale_row * gain

def reference(visual, w_key, w_value, key_gain, queries, grad_out, offsets, flips, lengths):
    visual_f = visual.astype(jnp.float32)
    total = jnp.zeros((COPIES, VIS, D), jnp.float32)
    live = (jnp.arange(TXT, dtype=jnp.int32)[None, :] < lengths[:, None]).astype(jnp.bfloat16)
    scale = HD ** (-0.5)
    for layer in range(LAYERS):
        for head in range(KV_HEADS):
            cols = slice(head * HD, (head + 1) * HD)
            qcols = slice(head * GROUP * HD, (head + 1) * GROUP * HD)
            wk = w_key[layer][:, cols].astype(jnp.float32)
            wv = w_value[layer][:, cols].astype(jnp.float32)
            gain = key_gain[layer, cols].astype(jnp.float32)
            kraw = jnp.einsum('cvd,dk->cvk', visual_f, wk)
            vraw = jnp.einsum('cvd,dk->cvk', visual_f, wv)
            normed, pull = jax.vjp(lambda raw: key_norm(raw, gain), kraw)
            keys = normed.astype(jnp.bfloat16).astype(jnp.float32)
            values = vraw.astype(jnp.bfloat16).astype(jnp.float32)
            query = queries[layer][:, :, qcols].reshape(COPIES, TXT, GROUP, HD).astype(jnp.float32)
            dout = (grad_out[layer][:, :, qcols] * live[:, :, None]).reshape(COPIES, TXT, GROUP, HD).astype(jnp.float32)
            scores = jnp.einsum('ctgd,cvd->cgtv', query, keys) * scale
            probs = jax.nn.softmax(scores, axis=-1)
            pb = probs.astype(jnp.bfloat16).astype(jnp.float32)
            dval = jnp.einsum('cgtv,ctgd->cvd', pb, dout)
            dprob = jnp.einsum('ctgd,cvd->cgtv', dout, values)
            dscore = probs * (dprob - lax.optimization_barrier(jnp.sum(probs * dprob, axis=-1, keepdims=True))) * scale
            dkey = jnp.einsum('cgtv,ctgd->cvd', dscore.astype(jnp.bfloat16).astype(jnp.float32), query)
            dkraw, = pull(dkey)
            term = jnp.einsum('cvk,dk->cvd', dkraw.astype(jnp.bfloat16).astype(jnp.float32), wk)
            term = term + jnp.einsum('cvk,dk->cvd', dval.astype(jnp.bfloat16).astype(jnp.float32), wv)
            rounded = lax.optimization_barrier(term.astype(jnp.bfloat16))
            total = total + rounded.astype(jnp.float32)
    grid = total.reshape(COPIES, GH, GW, D)
    base = jnp.zeros((GH, BW, D), jnp.float32)
    column = jnp.arange(GW, dtype=jnp.int32)
    for copy_index in range(COPIES):
        target = offsets[copy_index] + jnp.where(flips[copy_index] == 1, GW - 1 - column, column)
        base = base.at[:, target.astype(jnp.int32), :].add(grid[copy_index])
    return base.reshape(GH * BW, D)
```

```python
import jax
import jax.numpy as jnp
from jax import lax
from jax.sharding import Mesh, PartitionSpec as P

GW = 24
BW = 32
EPS = 1e-05
SECTION = ("zl", "core")
TENSOR = ("yh", "yl")
COPY = ("x", "zh")


def gather_rows(visual):
    shard = visual[0].reshape(1, 24, 1024)
    spread = jnp.broadcast_to(shard, (16, 24, 1024))
    same = lax.all_to_all(spread, ("zl", "yh"), 0, 0)
    same = same.reshape(48, 8192)
    up = [(y, (y + 1) % 8) for y in range(8)]
    down = [(y, (y - 1) % 8) for y in range(8)]
    low = lax.ppermute(same[:24], TENSOR, up)
    high = lax.ppermute(same[24:], TENSOR, down)
    swap = [(0, 1), (1, 0)]
    own = jnp.concatenate([same, low, high], axis=0)
    rows = jnp.concatenate([own, lax.ppermute(own, "core", swap)], axis=0)
    r = jnp.arange(192, dtype=jnp.int32)
    core = (lax.axis_index("core") + r // 96) % 2
    parity = (lax.axis_index("yl") + (r // 48) % 2) % 2
    zl = (r // 12) % 4
    yh = (r // 3) % 4
    line = zl * 2 + core
    column = (yh * 2 + parity) * 3 + r % 3
    return rows, line, column


def on_device(visual, w_key, w_value, key_gain, queries, grad_out, offsets, flips, lengths):
    key_mat = w_key[0]
    value_mat = w_value[0]
    head_size = key_mat.shape[1]
    rows, line, column = gather_rows(visual)
    kraw = jnp.dot(rows, key_mat, preferred_element_type=jnp.float32)
    vraw = jnp.dot(rows, value_mat, preferred_element_type=jnp.float32)
    values = vraw.astype(jnp.bfloat16)
    gain = key_gain[0].astype(jnp.float32)

    def normed_keys(raw):
        scale_row = lax.rsqrt(jnp.mean(raw * raw, axis=-1, keepdims=True) + EPS)
        return raw * scale_row * gain

    normed, pull = jax.vjp(normed_keys, kraw)
    keys = normed.astype(jnp.bfloat16)
    text_len = queries.shape[2]
    query = queries[0, 0].reshape(text_len, -1, head_size)
    scale = head_size ** (-0.5)
    live = (jnp.arange(text_len, dtype=jnp.int32) < lengths[0]).astype(jnp.bfloat16)
    dout = (grad_out[0, 0] * live[:, None]).reshape(text_len, -1, head_size)
    scores = jnp.einsum("tgd,vd->gtv", query, keys, preferred_element_type=jnp.float32) * scale
    probs = jax.nn.softmax(scores, axis=-1)
    weights = probs.astype(jnp.bfloat16)
    dval = jnp.einsum("gtv,tgd->vd", weights, dout, preferred_element_type=jnp.float32)
    dprob = jnp.einsum("tgd,vd->gtv", dout, values, preferred_element_type=jnp.float32)
    dscore = probs * (dprob - jnp.sum(probs * dprob, axis=-1, keepdims=True)) * scale
    dkey = jnp.einsum(
        "gtv,tgd->vd", dscore.astype(jnp.bfloat16), query, preferred_element_type=jnp.float32
    )
    (dkraw,) = pull(dkey)
    fac = jnp.concatenate([dkraw, dval], axis=1).astype(jnp.bfloat16)
    target = line * BW + offsets[0] + jnp.where(flips[0] == 1, GW - 1 - column, column)
    onehot = (jnp.arange(8 * BW, dtype=jnp.int32)[:, None] == target[None, :]).astype(jnp.bfloat16)
    placed = jnp.dot(onehot, fac, preferred_element_type=jnp.float32).astype(jnp.bfloat16)
    parts = lax.all_to_all(placed.reshape(8, BW, -1), COPY, 0, 0)
    summed = jnp.sum(parts.astype(jnp.float32), axis=0).astype(jnp.bfloat16)
    part = jnp.einsum("bk,dk->bd", summed[:, :head_size], key_mat, preferred_element_type=jnp.float32)
    part = part + jnp.einsum("bk,dk->bd", summed[:, head_size:], value_mat, preferred_element_type=jnp.float32)
    part = part.astype(jnp.bfloat16)
    cut = part.reshape(BW, 8, 4, 2, 128).transpose(3, 2, 1, 0, 4).reshape(2, 32, BW, 128)
    mine = lax.axis_index("core")
    keep = lax.dynamic_index_in_dim(cut, mine, 0, keepdims=False)
    give = lax.dynamic_index_in_dim(cut, 1 - mine, 0, keepdims=False)
    got = lax.ppermute(give, "core", [(0, 1), (1, 0)])
    pair = (keep.astype(jnp.float32) + got.astype(jnp.float32)).astype(jnp.bfloat16)
    pieces = lax.all_to_all(pair, ("zl", "yh", "yl"), 0, 0)
    total = jnp.sum(pieces.astype(jnp.float32), axis=0).astype(jnp.bfloat16)
    wide = lax.all_to_all(jnp.broadcast_to(total[None], (8, BW, 128)), SECTION, 0, 0)
    turn = [(s * 8 + c, c * 8 + s) for s in range(8) for c in range(8)]
    out = lax.ppermute(wide, SECTION + COPY, turn)
    return out.transpose(1, 0, 2).reshape(BW, 1024).astype(jnp.float32)


def solution(mesh):
    fine = Mesh(mesh.devices.reshape(4, 2, 4, 2, 4, 2), ("zl", "core", "yh", "yl", "x", "zh"))
    placed = (
        P(COPY, SECTION + TENSOR, None),
        P(SECTION, None, TENSOR),
        P(SECTION, None, TENSOR),
        P(SECTION, TENSOR),
        P(SECTION, COPY, None, TENSOR),
        P(SECTION, COPY, None, TENSOR),
        P(COPY),
        P(COPY),
        P(COPY),
    )
    return jax.shard_map(
        on_device, mesh=fine, in_specs=placed, out_specs=P(SECTION, TENSOR), check_vma=False
    )
```

```python
import functools

import jax
import jax.numpy as jnp
from jax import lax
from jax.experimental import pallas as pl
from jax.experimental.pallas import tpu as pltpu
from jax.sharding import Mesh, PartitionSpec as P

GW = 24
BW = 32
EPS = 1e-05
SECTION = ("zl", "core")
TENSOR = ("yh", "yl")
COPY = ("x", "zh")
STEP = 2048
SWAP = [(0, 1), (1, 0)]
NT = (((1,), (1,)), ((), ()))
F32 = jnp.float32
BF16 = jnp.bfloat16


def factors_kernel(
    length, target, same, other, far_same, far_other, w_key, w_value, gain, query, grad, out, late, rows, sems
):
    pieces = (same, other, far_same, far_other)

    def load(step, i):
        part = pl.ds(step * STEP, STEP)
        return pltpu.make_async_copy(pieces[i].at[:, part], rows.at[pl.ds(48 * i, 48), part], sems.at[step, i])

    def bring(step):
        part = pl.ds(step * STEP, STEP)
        return pltpu.make_async_copy(w_value.at[part, :], late.at[part, :], sems.at[step, 4])

    steps = 8192 // STEP
    for step in range(steps):
        bring(step).start()
        for i in range(4):
            load(step, i).start()
    both = jnp.zeros((192, 256), F32)
    for step in range(steps):
        part = pl.ds(step * STEP, STEP)
        for i in range(4):
            load(step, i).wait()
        bring(step).wait()
        mats = jnp.concatenate([w_key[part, :], late[part, :]], axis=1)
        both += jnp.dot(rows[:, part], mats, preferred_element_type=F32)
    kraw = both[:, :128]
    values = both[:, 128:].astype(BF16)
    scale_row = lax.rsqrt(jnp.mean(kraw * kraw, axis=1, keepdims=True) + EPS)
    gains = gain[...].astype(F32)
    keys = (kraw * scale_row * gains).astype(BF16)
    scale = 128 ** (-0.5)
    text = lax.broadcasted_iota(jnp.int32, (128, 128), 0)
    live = text < length[0]
    dval = jnp.zeros((192, 128), F32)
    dkey = jnp.zeros((192, 128), F32)
    for g in range(8):
        lanes = pl.ds(g * 128, 128)
        q = query[:, lanes]
        dout = jnp.where(live, grad[:, lanes].astype(F32), 0.0).astype(BF16)
        scores = lax.dot_general(keys, q, NT, preferred_element_type=F32) * scale
        dprob = lax.dot_general(values, dout, NT, preferred_element_type=F32)
        grown = jnp.exp(scores - jnp.max(scores, axis=0, keepdims=True))
        probs = grown / jnp.sum(grown, axis=0, keepdims=True)
        inner = jnp.sum(probs * dprob, axis=0, keepdims=True)
        dscore = probs * (dprob - inner) * scale
        dval += jnp.dot(probs.astype(BF16), dout, preferred_element_type=F32)
        dkey += jnp.dot(dscore.astype(BF16), q, preferred_element_type=F32)
    dn = dkey * gains
    dot_row = jnp.sum(dn * kraw, axis=1, keepdims=True) * (1.0 / 128)
    dkraw = dn * scale_row - kraw * (scale_row * scale_row * scale_row * dot_row)
    fac = jnp.concatenate([dkraw.astype(BF16), dval.astype(BF16)], axis=1)
    patch = lax.broadcasted_iota(jnp.int32, (256, 192), 0)
    onehot = (patch == target[...]).astype(F32).astype(BF16)
    out[...] = jnp.dot(onehot, fac, preferred_element_type=F32).astype(BF16)


def product_kernel(mine, parts, w_key, w_value, keep, give):
    total = jnp.zeros((BW, 256), F32)
    for c in range(8):
        total += parts[c].astype(F32)
    total = total.astype(BF16)
    first = mine[0] == 0
    for y in range(8):
        part = pl.ds(y * 1024, 1024)
        mats = jnp.concatenate([w_key[part, :], w_value[part, :]], axis=1)
        wide = lax.dot_general(total, mats, NT, preferred_element_type=F32)
        for zl in range(4):
            left = wide[:, zl * 256 : zl * 256 + 128]
            right = wide[:, zl * 256 + 128 : zl * 256 + 256]
            keep[zl * 8 + y] = jnp.where(first, left, right).astype(BF16)
            give[zl * 8 + y] = jnp.where(first, right, left).astype(BF16)


def in_hbm(array):
    return pltpu.with_memory_space_constraint(array, pltpu.HBM)


def call(kernel, scalars, arrays, out_shape, limit, flops, kept=(), scratch=()):
    smem = pl.BlockSpec(memory_space=pltpu.SMEM)
    vmem = pl.BlockSpec(memory_space=pltpu.VMEM)
    whole = pl.BlockSpec(memory_space=pltpu.HBM)
    return pl.pallas_call(
        kernel,
        in_specs=[smem] * len(scalars) + [whole if i in kept else vmem for i in range(len(arrays))],
        out_specs=jax.tree.map(lambda _: vmem, out_shape),
        out_shape=out_shape,
        scratch_shapes=list(scratch),
        compiler_params=pltpu.CompilerParams(vmem_limit_bytes=limit),
        cost_estimate=pl.CostEstimate(flops=flops, bytes_accessed=8 << 20, transcendentals=0),
    )(*scalars, *arrays)


def on_device(visual, w_key, w_value, key_gain, queries, grad_out, offsets, flips, lengths):
    core = lax.axis_index("core")
    spread = jnp.broadcast_to(visual[0].reshape(1, 24, 1024), (16, 24, 1024))
    same = lax.all_to_all(spread, ("zl", "yh"), 0, 0).reshape(48, 8192)
    walk = [(k * 8 + (y + 1 - 2 * k) % 8, k * 8 + y) for k in range(2) for y in range(8)]
    other = lax.ppermute(same, ("core",) + TENSOR, walk)
    far_same = lax.ppermute(same, "core", SWAP)
    far_other = lax.ppermute(other, "core", SWAP)
    rows = [same, other, far_same, far_other]
    r = jnp.arange(192, dtype=jnp.int32)
    line = ((r // 12) % 4) * 2 + (core + r // 96) % 2
    parity = (lax.axis_index("yl") + (r // 48) % 2) % 2
    column = (((r // 3) % 4) * 2 + parity) * 3 + r % 3
    target = line * BW + offsets[0] + jnp.where(flips[0] == 1, GW - 1 - column, column)
    key_mat, value_mat = w_key[0], w_value[0]
    placed, value_mat = call(
        factors_kernel,
        [lengths],
        [target[None], *map(in_hbm, rows), key_mat, in_hbm(value_mat), key_gain, queries[0, 0], grad_out[0, 0]],
        (jax.ShapeDtypeStruct((256, 256), BF16), jax.ShapeDtypeStruct((8192, 128), BF16)),
        12 << 20,
        1 << 30,
        kept=(1, 2, 3, 4, 6),
        scratch=[pltpu.VMEM((192, 8192), BF16), pltpu.SemaphoreType.DMA((8192 // STEP, 5))],
    )
    parts = lax.all_to_all(placed.reshape(8, BW, 256), COPY, 0, 0)
    block = jax.ShapeDtypeStruct((32, BW, 128), BF16)
    keep, give = call(
        product_kernel, [core.astype(jnp.int32)[None]], [parts, key_mat, value_mat], (block, block), 8 << 20, 1 << 27
    )
    got = lax.ppermute(give, "core", SWAP)
    pair = (keep.astype(F32) + got.astype(F32)).astype(BF16)
    pieces = lax.all_to_all(pair, ("zl",) + TENSOR, 0, 0)
    total = jnp.sum(pieces.astype(F32), axis=0).astype(BF16)
    wide = lax.all_to_all(jnp.broadcast_to(total[None], (8, BW, 128)), SECTION, 0, 0)
    out = lax.ppermute(wide, SECTION + COPY, turn())
    return out.transpose(1, 0, 2).reshape(BW, 1024).astype(F32)


def turn():
    pairs = []
    for row in range(8):
        x, zh = row // 2, row % 2
        senders = sorted(range(8), key=lambda s: abs(s // 2 - x))
        for side in range(2):
            along = lambda s: abs(s // 2 - x) if side == 0 else 4 - abs(s // 2 - x)
            order = sorted(senders[4 * side : 4 * side + 4], key=along)
            close = sorted(range(4), key=lambda other: -min((other - x) % 4, (x - other) % 4))
            for s, to_x in zip(order, close):
                pairs.append((s * 8 + row, row * 8 + to_x * 2 + (zh ^ side)))
    return pairs


def solution(mesh):
    fine = Mesh(mesh.devices.reshape(4, 2, 4, 2, 4, 2), ("zl", "core", "yh", "yl", "x", "zh"))
    placed = (
        P(COPY, SECTION + TENSOR, None),
        P(SECTION, None, TENSOR),
        P(SECTION, None, TENSOR),
        P(SECTION, TENSOR),
        P(SECTION, COPY, None, TENSOR),
        P(SECTION, COPY, None, TENSOR),
        P(COPY),
        P(COPY),
        P(COPY),
    )
    return jax.shard_map(
        on_device, mesh=fine, in_specs=placed, out_specs=P(SECTION, TENSOR), check_vma=False
    )
```

```python
import functools

import jax
import jax.numpy as jnp
from jax import lax
from jax.experimental import pallas as pl
from jax.experimental.pallas import tpu as pltpu
from jax.sharding import Mesh, PartitionSpec as P

GW = 24
BW = 32
EPS = 1e-05
SECTION = ("zl", "core")
TENSOR = ("yh", "yl")
COPY = ("x", "zh")
STEP = 2048
SWAP = [(0, 1), (1, 0)]
NT = (((1,), (1,)), ((), ()))
F32 = jnp.float32
BF16 = jnp.bfloat16


def factors_kernel(length, target, same, other, far_same, far_other, w_key, w_value, gain, query, grad, out):
    pieces = (same, other, far_same, far_other)
    both = jnp.zeros((192, 256), F32)
    for start in range(0, 8192, STEP):
        part = pl.ds(start, STEP)
        rows = jnp.concatenate([piece[:, part] for piece in pieces], axis=0)
        mats = jnp.concatenate([w_key[part, :], w_value[part, :]], axis=1)
        both += jnp.dot(rows, mats, preferred_element_type=F32)
    kraw = both[:, :128]
    values = both[:, 128:].astype(BF16)
    scale_row = lax.rsqrt(jnp.mean(kraw * kraw, axis=1, keepdims=True) + EPS)
    gains = gain[...].astype(F32)
    keys = (kraw * scale_row * gains).astype(BF16)
    scale = 128 ** (-0.5)
    text = lax.broadcasted_iota(jnp.int32, (128, 128), 0)
    live = text < length[0]
    dval = jnp.zeros((192, 128), F32)
    dkey = jnp.zeros((192, 128), F32)
    for g in range(8):
        lanes = pl.ds(g * 128, 128)
        q = query[:, lanes]
        dout = jnp.where(live, grad[:, lanes].astype(F32), 0.0).astype(BF16)
        scores = lax.dot_general(keys, q, NT, preferred_element_type=F32) * scale
        dprob = lax.dot_general(values, dout, NT, preferred_element_type=F32)
        grown = jnp.exp(scores - jnp.max(scores, axis=0, keepdims=True))
        probs = grown / jnp.sum(grown, axis=0, keepdims=True)
        inner = jnp.sum(probs * dprob, axis=0, keepdims=True)
        dscore = probs * (dprob - inner) * scale
        dval += jnp.dot(probs.astype(BF16), dout, preferred_element_type=F32)
        dkey += jnp.dot(dscore.astype(BF16), q, preferred_element_type=F32)
    dn = dkey * gains
    dot_row = jnp.sum(dn * kraw, axis=1, keepdims=True) * (1.0 / 128)
    dkraw = dn * scale_row - kraw * (scale_row * scale_row * scale_row * dot_row)
    fac = jnp.concatenate([dkraw.astype(BF16), dval.astype(BF16)], axis=1)
    patch = lax.broadcasted_iota(jnp.int32, (256, 192), 0)
    onehot = (patch == target[...]).astype(F32).astype(BF16)
    out[...] = jnp.dot(onehot, fac, preferred_element_type=F32).astype(BF16)


def bring_kernel(after, weights, out, sem):
    copy = pltpu.make_async_copy(weights, out, sem)
    copy.start()
    copy.wait()


def product_kernel(mine, parts, w_key, w_value, keep, give):
    total = jnp.zeros((BW, 256), F32)
    for c in range(8):
        total += parts[c].astype(F32)
    total = total.astype(BF16)
    first = mine[0] == 0
    for y in range(8):
        part = pl.ds(y * 1024, 1024)
        mats = jnp.concatenate([w_key[part, :], w_value[part, :]], axis=1)
        wide = lax.dot_general(total, mats, NT, preferred_element_type=F32)
        for zl in range(4):
            left = wide[:, zl * 256 : zl * 256 + 128]
            right = wide[:, zl * 256 + 128 : zl * 256 + 256]
            keep[zl * 8 + y] = jnp.where(first, left, right).astype(BF16)
            give[zl * 8 + y] = jnp.where(first, right, left).astype(BF16)


def in_hbm(array):
    return pltpu.with_memory_space_constraint(array, pltpu.HBM)


def call(kernel, scalars, arrays, out_shape, limit, flops, kept=(), scratch=()):
    smem = pl.BlockSpec(memory_space=pltpu.SMEM)
    vmem = pl.BlockSpec(memory_space=pltpu.VMEM)
    whole = pl.BlockSpec(memory_space=pl.ANY)
    return pl.pallas_call(
        kernel,
        in_specs=[smem] * len(scalars) + [whole if i in kept else vmem for i in range(len(arrays))],
        out_specs=jax.tree.map(lambda _: vmem, out_shape),
        out_shape=out_shape,
        scratch_shapes=list(scratch),
        compiler_params=pltpu.CompilerParams(vmem_limit_bytes=limit),
        cost_estimate=pl.CostEstimate(flops=flops, bytes_accessed=8 << 20, transcendentals=0),
    )(*scalars, *arrays)


def on_device(visual, w_key, w_value, key_gain, queries, grad_out, offsets, flips, lengths):
    core = lax.axis_index("core")
    spread = jnp.broadcast_to(visual[0].reshape(1, 24, 1024), (16, 24, 1024))
    same = lax.all_to_all(spread, ("zl", "yh"), 0, 0).reshape(48, 8192)
    walk = [(k * 8 + (y + 1 - 2 * k) % 8, k * 8 + y) for k in range(2) for y in range(8)]
    other = lax.ppermute(same, ("core",) + TENSOR, walk)
    far_same = lax.ppermute(same, "core", SWAP)
    far_other = lax.ppermute(other, "core", SWAP)
    rows = [same, other, far_same, far_other]
    r = jnp.arange(192, dtype=jnp.int32)
    line = ((r // 12) % 4) * 2 + (core + r // 96) % 2
    parity = (lax.axis_index("yl") + (r // 48) % 2) % 2
    column = (((r // 3) % 4) * 2 + parity) * 3 + r % 3
    target = line * BW + offsets[0] + jnp.where(flips[0] == 1, GW - 1 - column, column)
    key_mat, value_mat = w_key[0], w_value[0]
    value_mat = call(
        bring_kernel,
        [],
        [other, in_hbm(value_mat)],
        jax.ShapeDtypeStruct((8192, 128), BF16),
        1 << 20,
        1 << 20,
        kept=(0, 1),
        scratch=[pltpu.SemaphoreType.DMA],
    )
    placed = call(
        factors_kernel,
        [lengths],
        [target[None], *rows, key_mat, value_mat, key_gain, queries[0, 0], grad_out[0, 0]],
        jax.ShapeDtypeStruct((256, 256), BF16),
        12 << 20,
        1 << 30,
    )
    parts = lax.all_to_all(placed.reshape(8, BW, 256), COPY, 0, 0)
    block = jax.ShapeDtypeStruct((32, BW, 128), BF16)
    keep, give = call(
        product_kernel, [core.astype(jnp.int32)[None]], [parts, key_mat, value_mat], (block, block), 8 << 20, 1 << 27
    )
    got = lax.ppermute(give, "core", SWAP)
    pair = (keep.astype(F32) + got.astype(F32)).astype(BF16)
    pieces = lax.all_to_all(pair, ("zl",) + TENSOR, 0, 0)
    total = jnp.sum(pieces.astype(F32), axis=0).astype(BF16)
    wide = lax.all_to_all(jnp.broadcast_to(total[None], (8, BW, 128)), SECTION, 0, 0)
    out = lax.ppermute(wide, SECTION + COPY, turn())
    return out.transpose(1, 0, 2).reshape(BW, 1024).astype(F32)


def turn():
    pairs = []
    for row in range(8):
        x, zh = row // 2, row % 2
        senders = sorted(range(8), key=lambda s: abs(s // 2 - x))
        for side in range(2):
            along = lambda s: abs(s // 2 - x) if side == 0 else 4 - abs(s // 2 - x)
            order = sorted(senders[4 * side : 4 * side + 4], key=along)
            close = sorted(range(4), key=lambda other: -min((other - x) % 4, (x - other) % 4))
            for s, to_x in zip(order, close):
                pairs.append((s * 8 + row, row * 8 + to_x * 2 + (zh ^ side)))
    return pairs


def solution(mesh):
    fine = Mesh(mesh.devices.reshape(4, 2, 4, 2, 4, 2), ("zl", "core", "yh", "yl", "x", "zh"))
    placed = (
        P(COPY, SECTION + TENSOR, None),
        P(SECTION, None, TENSOR),
        P(SECTION, None, TENSOR),
        P(SECTION, TENSOR),
        P(SECTION, COPY, None, TENSOR),
        P(SECTION, COPY, None, TENSOR),
        P(COPY),
        P(COPY),
        P(COPY),
    )
    return jax.shard_map(
        on_device, mesh=fine, in_specs=placed, out_specs=P(SECTION, TENSOR), check_vma=False
    )
```

```python
import functools

import jax
import jax.numpy as jnp
from jax import lax
from jax.experimental import pallas as pl
from jax.experimental.pallas import tpu as pltpu
from jax.sharding import Mesh, PartitionSpec as P

GW = 24
BW = 32
EPS = 1e-05
SECTION = ("zl", "core")
TENSOR = ("yh", "yl")
COPY = ("x", "zh")
STEP = 2048
SWAP = [(0, 1), (1, 0)]
NT = (((1,), (1,)), ((), ()))
F32 = jnp.float32
BF16 = jnp.bfloat16


def factors_kernel(length, target, same, other, far_same, far_other, w_key, w_value, gain, query, grad, out):
    pieces = (same, other, far_same, far_other)
    both = jnp.zeros((192, 256), F32)
    for start in range(0, 8192, STEP):
        part = pl.ds(start, STEP)
        rows = jnp.concatenate([piece[:, part] for piece in pieces], axis=0)
        mats = jnp.concatenate([w_key[part, :], w_value[part, :]], axis=1)
        both += jnp.dot(rows, mats, preferred_element_type=F32)
    kraw = both[:, :128]
    values = both[:, 128:].astype(BF16)
    scale_row = lax.rsqrt(jnp.mean(kraw * kraw, axis=1, keepdims=True) + EPS)
    gains = gain[...].astype(F32)
    keys = (kraw * scale_row * gains).astype(BF16)
    scale = 128 ** (-0.5)
    text = lax.broadcasted_iota(jnp.int32, (128, 128), 0)
    live = text < length[0]
    dval = jnp.zeros((192, 128), F32)
    dkey = jnp.zeros((192, 128), F32)
    for g in range(8):
        lanes = pl.ds(g * 128, 128)
        q = query[:, lanes]
        dout = jnp.where(live, grad[:, lanes].astype(F32), 0.0).astype(BF16)
        scores = lax.dot_general(keys, q, NT, preferred_element_type=F32) * scale
        dprob = lax.dot_general(values, dout, NT, preferred_element_type=F32)
        grown = jnp.exp(scores - jnp.max(scores, axis=0, keepdims=True))
        probs = grown / jnp.sum(grown, axis=0, keepdims=True)
        inner = jnp.sum(probs * dprob, axis=0, keepdims=True)
        dscore = probs * (dprob - inner) * scale
        dval += jnp.dot(probs.astype(BF16), dout, preferred_element_type=F32)
        dkey += jnp.dot(dscore.astype(BF16), q, preferred_element_type=F32)
    dn = dkey * gains
    dot_row = jnp.sum(dn * kraw, axis=1, keepdims=True) * (1.0 / 128)
    dkraw = dn * scale_row - kraw * (scale_row * scale_row * scale_row * dot_row)
    fac = jnp.concatenate([dkraw.astype(BF16), dval.astype(BF16)], axis=1)
    patch = lax.broadcasted_iota(jnp.int32, (256, 192), 0)
    onehot = (patch == target[...]).astype(F32).astype(BF16)
    out[...] = jnp.dot(onehot, fac, preferred_element_type=F32).astype(BF16)


def bring_kernel(after, weights, out, sem):
    copy = pltpu.make_async_copy(weights, out, sem)
    copy.start()
    copy.wait()


def product_kernel(mine, parts, w_key, w_value, keep, give):
    total = jnp.zeros((BW, 256), F32)
    for c in range(8):
        total += parts[c].astype(F32)
    total = total.astype(BF16)
    first = mine[0] == 0
    for y in range(8):
        part = pl.ds(y * 1024, 1024)
        mats = jnp.concatenate([w_key[part, :], w_value[part, :]], axis=1)
        wide = lax.dot_general(total, mats, NT, preferred_element_type=F32)
        for zl in range(4):
            left = wide[:, zl * 256 : zl * 256 + 128]
            right = wide[:, zl * 256 + 128 : zl * 256 + 256]
            keep[zl * 8 + y] = jnp.where(first, left, right).astype(BF16)
            give[zl * 8 + y] = jnp.where(first, right, left).astype(BF16)


def in_hbm(array):
    return pltpu.with_memory_space_constraint(array, pltpu.HBM)


def call(kernel, scalars, arrays, out_shape, limit, flops, kept=(), scratch=()):
    smem = pl.BlockSpec(memory_space=pltpu.SMEM)
    vmem = pl.BlockSpec(memory_space=pltpu.VMEM)
    whole = pl.BlockSpec(memory_space=pl.ANY)
    return pl.pallas_call(
        kernel,
        in_specs=[smem] * len(scalars) + [whole if i in kept else vmem for i in range(len(arrays))],
        out_specs=jax.tree.map(lambda _: vmem, out_shape),
        out_shape=out_shape,
        scratch_shapes=list(scratch),
        compiler_params=pltpu.CompilerParams(vmem_limit_bytes=limit),
        cost_estimate=pl.CostEstimate(flops=flops, bytes_accessed=8 << 20, transcendentals=0),
    )(*scalars, *arrays)


def on_device(visual, w_key, w_value, key_gain, queries, grad_out, offsets, flips, lengths):
    core = lax.axis_index("core")
    spread = jnp.broadcast_to(visual[0].reshape(1, 24, 1024), (16, 24, 1024))
    same = lax.all_to_all(spread, ("zl", "yh"), 0, 0).reshape(48, 8192)
    walk = [(k * 8 + (y + 1 - 2 * k) % 8, k * 8 + y) for k in range(2) for y in range(8)]
    other = lax.ppermute(same, ("core",) + TENSOR, walk)
    far_same = lax.ppermute(same, "core", SWAP)
    r = jnp.arange(192, dtype=jnp.int32)
    line = ((r // 12) % 4) * 2 + (core + r // 96) % 2
    parity = (lax.axis_index("yl") + (r // 48) % 2) % 2
    column = (((r // 3) % 4) * 2 + parity) * 3 + r % 3
    target = line * BW + offsets[0] + jnp.where(flips[0] == 1, GW - 1 - column, column)
    other, target, lengths = lax.optimization_barrier((other, target, lengths))
    far_other = lax.ppermute(other, "core", SWAP)
    rows = [same, other, far_same, far_other]
    key_mat, value_mat = w_key[0], w_value[0]
    value_mat = call(
        bring_kernel,
        [],
        [other, in_hbm(value_mat)],
        jax.ShapeDtypeStruct((8192, 128), BF16),
        1 << 20,
        1 << 20,
        kept=(0, 1),
        scratch=[pltpu.SemaphoreType.DMA],
    )
    placed = call(
        factors_kernel,
        [lengths],
        [target[None], *rows, key_mat, value_mat, key_gain, queries[0, 0], grad_out[0, 0]],
        jax.ShapeDtypeStruct((256, 256), BF16),
        12 << 20,
        1 << 30,
    )
    parts = lax.all_to_all(placed.reshape(8, BW, 256), COPY, 0, 0)
    block = jax.ShapeDtypeStruct((32, BW, 128), BF16)
    keep, give = call(
        product_kernel, [core.astype(jnp.int32)[None]], [parts, key_mat, value_mat], (block, block), 8 << 20, 1 << 27
    )
    got = lax.ppermute(give, "core", SWAP)
    pair = (keep.astype(F32) + got.astype(F32)).astype(BF16)
    pieces = lax.all_to_all(pair, ("zl",) + TENSOR, 0, 0)
    total = jnp.sum(pieces.astype(F32), axis=0).astype(BF16)
    wide = lax.all_to_all(jnp.broadcast_to(total[None], (8, BW, 128)), SECTION, 0, 0)
    out = lax.ppermute(wide, SECTION + COPY, turn())
    return out.transpose(1, 0, 2).reshape(BW, 1024).astype(F32)


def turn():
    pairs = []
    for row in range(8):
        x, zh = row // 2, row % 2
        senders = sorted(range(8), key=lambda s: abs(s // 2 - x))
        for side in range(2):
            along = lambda s: abs(s // 2 - x) if side == 0 else 4 - abs(s // 2 - x)
            order = sorted(senders[4 * side : 4 * side + 4], key=along)
            close = sorted(range(4), key=lambda other: -min((other - x) % 4, (x - other) % 4))
            for s, to_x in zip(order, close):
                pairs.append((s * 8 + row, row * 8 + to_x * 2 + (zh ^ side)))
    return pairs


def solution(mesh):
    fine = Mesh(mesh.devices.reshape(4, 2, 4, 2, 4, 2), ("zl", "core", "yh", "yl", "x", "zh"))
    placed = (
        P(COPY, SECTION + TENSOR, None),
        P(SECTION, None, TENSOR),
        P(SECTION, None, TENSOR),
        P(SECTION, TENSOR),
        P(SECTION, COPY, None, TENSOR),
        P(SECTION, COPY, None, TENSOR),
        P(COPY),
        P(COPY),
        P(COPY),
    )
    return jax.shard_map(
        on_device, mesh=fine, in_specs=placed, out_specs=P(SECTION, TENSOR), check_vma=False
    )
```
